32 devices in a mesh: fsdp: 4 (over z), ctx: 2 (over y), tp: 4 (over x, core).
Axes of the slice: x: 2, y: 2, z: 4, core: 2. Of those that a mesh axis runs over, the one named last changes fastest.
Arguments:
- tokens: bfloat16 [4096, 1536], P(('fsdp', 'ctx')), may hold values from -6 to 6
- w_query: bfloat16 [2, 1536, 1536], P(None, 'fsdp', 'tp'), may hold values from -1 to 1
- w_key: bfloat16 [2, 1536, 768], P(None, 'fsdp', 'tp'), may hold values from -1 to 1
- w_value: bfloat16 [2, 1536, 768], P(None, 'fsdp', 'tp'), may hold values from -0.15625 to 0.15625
- w_out: bfloat16 [2, 1536, 1536], P(None, 'tp', 'fsdp'), may hold values from -0.625 to 0.625
- w_gate: bfloat16 [2, 1536, 4096], P(None, 'fsdp', 'tp'), may hold values from -0.15625 to 0.15625
- w_up: bfloat16 [2, 1536, 4096], P(None, 'fsdp', 'tp'), may hold values from -0.15625 to 0.15625
- w_down: bfloat16 [2, 4096, 1536], P(None, 'tp', 'fsdp'), may hold values from -0.1875 to 0.1875
- gain_attn: bfloat16 [2, 1536], P(None, 'fsdp'), may hold values from 0.25 to 1.75
- gain_mlp: bfloat16 [2, 1536], P(None, 'fsdp'), may hold values from 0.25 to 1.75
- cotangent: bfloat16 [4096, 1536], P(('fsdp', 'ctx')), may hold values from -6 to 6
- piece_table: int32 [4, 8], replicated, may hold values from 0 to 7, each once within a row
- seq_lengths: int32 [4, 4], replicated, may hold values from 1 to 512, 1024 in all within a row
Outputs:
- output: bfloat16 [4096, 1536], P(('fsdp', 'ctx'))
- input_grad: float32 [4096, 1536], P(('fsdp', 'ctx'))
- grad_query: float32 [2, 1536, 1536], P(None, 'fsdp', 'tp')
- grad_key: float32 [2, 1536, 768], P(None, 'fsdp', 'tp')
- grad_value: float32 [2, 1536, 768], P(None, 'fsdp', 'tp')
- grad_out: float32 [2, 1536, 1536], P(None, 'tp', 'fsdp')
- grad_gate: float32 [2, 1536, 4096], P(None, 'fsdp', 'tp')
- grad_up: float32 [2, 1536, 4096], P(None, 'fsdp', 'tp')
- grad_down: float32 [2, 4096, 1536], P(None, 'tp', 'fsdp')
- grad_gain_attn: float32 [2, 1536], P(None, 'fsdp')
- grad_gain_mlp: float32 [2, 1536], P(None, 'fsdp')
The draws below stay inside these ranges and needn't reach their ends.
Inputs may be any that keep to these rules, and one draw needn't show every extreme that they name: `piece_table`: row f names each stored slot once; slot s is piece s % 4 of device s // 4 along ctx in group f. `seq_lengths`: row f holds the lengths of the 4 sequences packed one after another in logical order in group f; they sum to 1024 and the largest is 512.
All inputs are finite; a program needn't handle non-finite values.
Results may differ from the reference program's by a relative error of at most 0.03.
The reference program's roundings to bfloat16 on the way count: a program that leaves them out, or rounds other values in their place, can miss the bound.
Values may be sent and summed in bfloat16 or wider, within the bound.
No kernel may reach another device: no remote copies, remote signals or barrier semaphores. Data moves between devices by JAX's collectives and lax.ppermute only.
A program may use at most 256 MiB of HBM per device.

```python
import math
import jax
import jax.numpy as jnp
import numpy as np
from jax import lax

D = 1536
H = 16
KV = 8
HD = 96
FF = 4096
LAYERS = 2
PIECE = 128
GROUP_TOK = 1024
PIECES_GROUP = 8
TOKENS = 4096
MAXLEN = 512
NSEQ = 4
N_FSDP = 4


def base_weight(key, salt, columns):
    sampled = jax.random.normal(jax.random.fold_in(key, salt), (LAYERS, D, columns), jnp.float32)
    return jnp.clip(sampled, -6.0, 6.0) / math.sqrt(D)


def draw_w_query(key, part):
    drawn = base_weight(key, 21, H * HD)
    return jnp.clip(drawn, -1.0, 1.0).astype(jnp.bfloat16)


def draw_w_key(key, part):
    drawn = base_weight(key, 22, KV * HD)
    return jnp.clip(drawn, -1.0, 1.0).astype(jnp.bfloat16)


def draw_tokens(key, part):
    sampled = jnp.clip(jax.random.normal(jax.random.fold_in(key, 11), (TOKENS, D), jnp.float32), -6.0, 6.0)
    return sampled.astype(jnp.bfloat16)


def block_levels(key, extent, pieces, smallest, top_value):
    factor_of = 1.0
    for dim, shards_of in pieces:
        steps = jax.random.uniform(jax.random.fold_in(jax.random.fold_in(key, 6), dim), (shards_of,), jnp.float32, smallest / len(pieces), top_value / len(pieces))
        factor_of = factor_of * jnp.repeat(jnp.exp(steps), extent[dim] // shards_of).reshape((-1,) + (1,) * (len(extent) - 1 - dim))
    return factor_of


def profile(count, total, reach, slope):
    weights = [(1 << 20) // math.isqrt(standing ** slope) + 1 for standing in range(2, count + 1)]
    spare, counts = total - reach - (count - 1), [1] * (count - 1)
    while spare > 0:
        free = [i for i in range(count - 1) if counts[i] < reach]
        pool, left = sum([weights[i] for i in free]), spare
        for i in free:
            addition = min(reach - counts[i], max(1, left * weights[i] // pool), spare)
            counts[i] = counts[i] + addition
            spare = spare - addition
    return np.array([reach] + counts)


def ragged_sizes(rng, count, total, most, slope):
    if count == 2:
        one = jax.random.randint(rng, (), max(1, total - most), min(most, total - 1) + 1)
        return jnp.stack([one, total - one])
    tallies = jnp.asarray(profile(count, total, most, slope), jnp.int32)
    couples = (count - 1) // 2
    donor, receiver = tallies[1:1 + 2 * couples:2], tallies[2:2 + 2 * couples:2]
    room = jnp.minimum(donor - 1, most - receiver)
    moved = jax.random.randint(jax.random.fold_in(rng, 1), (couples,), 0, 1 << 20) % (room + 1)
    tallies = tallies.at[1:1 + 2 * couples:2].set(donor - moved).at[2:2 + 2 * couples:2].set(receiver + moved)
    return tallies[jax.random.permutation(jax.random.fold_in(rng, 2), count)]


def noise(key, shape, spread, reach, split=(), kind=jnp.bfloat16):
    level = block_levels(key, shape, split, -0.22, 0.18) if split else 1.0
    values = jax.random.normal(key, shape, jnp.float32) * spread * level
    return jnp.minimum(jnp.maximum(values, -reach), reach).astype(kind)


def setup_inputs(seed: int = 0) -> dict:
    splits = jax.random.split(jax.random.key(seed), 14)
    tokens = draw_tokens(jax.random.fold_in(splits[13], 71), 0)
    w_query = draw_w_query(jax.random.fold_in(splits[13], 71), 0)
    w_key = draw_w_key(jax.random.fold_in(splits[13], 71), 0)
    w_value = noise(splits[3], (LAYERS, D, KV * HD), D ** -0.5, 0.15625, ((1, 4), (2, 4)))
    w_out = noise(splits[4], (LAYERS, H * HD, D), (H * HD // 16) ** -0.5, 0.625, ((1, 4), (2, 4)))
    w_gate = noise(splits[5], (LAYERS, D, FF), D ** -0.5, 0.15625, ((1, 4), (2, 4)))
    w_up = noise(splits[6], (LAYERS, D, FF), D ** -0.5, 0.15625, ((1, 4), (2, 4)))
    w_down = noise(splits[7], (LAYERS, FF, D), (FF // 4) ** -0.5, 0.1875, ((1, 4), (2, 4)))
    gain_attn = jnp.clip(1.0 + 0.15 * jax.random.normal(splits[8], (LAYERS, D), jnp.float32), 0.25, 1.75).astype(jnp.bfloat16)
    gain_mlp = jnp.clip(1.0 + 0.15 * jax.random.normal(splits[9], (LAYERS, D), jnp.float32), 0.25, 1.75).astype(jnp.bfloat16)
    cotangent = noise(splits[10], (TOKENS, D), 1.0, 6.0, ((0, 8),))
    piece_table = jax.vmap(lambda own: jax.random.permutation(own, PIECES_GROUP))(jax.random.split(splits[11], N_FSDP)).reshape((N_FSDP, PIECES_GROUP)).astype(jnp.int32)
    seq_lengths = jax.vmap(lambda own: ragged_sizes(own, NSEQ, GROUP_TOK, MAXLEN, 2))(jax.random.split(splits[12], N_FSDP)).reshape((N_FSDP, NSEQ)).astype(jnp.int32)
    return dict(tokens=tokens, w_query=w_query, w_key=w_key, w_value=w_value, w_out=w_out, w_gate=w_gate, w_up=w_up, w_down=w_down, gain_attn=gain_attn, gain_mlp=gain_mlp, cotangent=cotangent, piece_table=piece_table, seq_lengths=seq_lengths)


EPS = 1e-05
THETA = 100000.0
NEG = -1e+30

def layout(table_row, length_row):
    count = table_row.shape[0]
    slot_ids = jnp.arange(count, dtype=jnp.int32)
    owners = lax.optimization_barrier(jnp.sum(jnp.where(table_row[:, None] == slot_ids[None, :], slot_ids[:, None], 0), axis=0)).astype(jnp.int32)
    row_ids = jnp.arange(count * PIECE, dtype=jnp.int32)
    piece_of = row_ids // PIECE
    logical = lax.optimization_barrier(jnp.sum(jnp.where(piece_of[:, None] == slot_ids[None, :], owners[None, :], 0), axis=1)).astype(jnp.int32) * PIECE + row_ids % PIECE
    seq_ends = jnp.cumsum(length_row).astype(jnp.int32)
    passed = logical[:, None] >= seq_ends[None, :]
    sequence = lax.optimization_barrier(jnp.sum(passed.astype(jnp.int32), axis=1)).astype(jnp.int32)
    position = (logical - lax.optimization_barrier(jnp.sum(jnp.where(passed, length_row[None, :], 0), axis=1))).astype(jnp.int32)
    return (logical, sequence, position)

def rotate(values, position, direction):
    row_count = values.shape[0]
    head_count = values.shape[1] // HD
    half_width = HD // 2
    frequency = jnp.exp(jnp.arange(half_width, dtype=jnp.float32) * (-2.0 * math.log(THETA) / HD))
    angles = position.astype(jnp.float32)[:, None] * frequency[None, :]
    cosine = jnp.cos(angles)[:, None, :]
    sine_part = direction * jnp.sin(angles)[:, None, :]
    shaped = values.reshape(row_count, head_count, HD)
    leading = shaped[..., :half_width]
    trailing = shaped[..., half_width:]
    return jnp.concatenate([leading * cosine - trailing * sine_part, leading * sine_part + trailing * cosine], axis=-1).reshape(row_count, head_count * HD)

def product(left, right):
    return jnp.dot(left, right, preferred_element_type=jnp.float32)

def outer_sum(left, right):
    return lax.dot_general(left, right, (((0,), (0,)), ((), ())), preferred_element_type=jnp.float32)

def transposed(left, right):
    return lax.dot_general(left, right, (((1,), (1,)), ((), ())), preferred_element_type=jnp.float32)

def split_heads(query, key, value):
    row_count = query.shape[0]
    key_count = key.shape[0]
    groups = key.shape[1] // HD
    shared = H // KV
    query_heads = query.reshape(row_count, groups, shared, HD).transpose(1, 2, 0, 3)
    key_heads = key.reshape(key_count, groups, HD).transpose(1, 0, 2)
    value_heads = value.reshape(key_count, groups, HD).transpose(1, 0, 2)
    return (query_heads, key_heads, value_heads)

def attend(query, key, value, allowed):
    row_count = query.shape[0]
    score_scale = 1.0 / math.sqrt(HD)
    query_heads, key_heads, value_heads = split_heads(query, key, value)

    def per_head(operands):
        query_one, key_one, value_one = operands
        scores = jnp.einsum('rqd,kd->rqk', query_one.astype(jnp.float32), key_one.astype(jnp.float32)) * score_scale
        scores = jnp.where(allowed[None], scores, NEG)
        row_max = lax.optimization_barrier(jnp.max(scores, axis=-1, keepdims=True))
        log_total = row_max + jnp.log(lax.optimization_barrier(jnp.sum(jnp.exp(scores - row_max), axis=-1, keepdims=True)))
        probabilities = jnp.exp(scores - log_total).astype(jnp.bfloat16)
        result = jnp.einsum('rqk,kd->rqd', probabilities.astype(jnp.float32), value_one.astype(jnp.float32))
        return (result.astype(jnp.bfloat16), log_total[..., 0])
    attended, log_total = lax.map(per_head, (query_heads, key_heads, value_heads))
    return (attended.transpose(2, 0, 1, 3).reshape(row_count, -1), log_total)

def attend_back(query, key, value, allowed, log_total, grad_attended):
    row_count = query.shape[0]
    key_count = key.shape[0]
    score_scale = 1.0 / math.sqrt(HD)
    query_heads, key_heads, value_heads = split_heads(query, key, value)
    grad_heads = grad_attended.reshape(row_count, key.shape[1] // HD, H // KV, HD).transpose(1, 2, 0, 3)

    def per_head(operands):
        query_one, key_one, value_one, total_one, grad_one = operands
        scores = jnp.einsum('rqd,kd->rqk', query_one.astype(jnp.float32), key_one.astype(jnp.float32)) * score_scale
        scores = jnp.where(allowed[None], scores, NEG)
        probabilities = jnp.exp(scores - total_one[..., None])
        grad_prob = jnp.einsum('rqd,kd->rqk', grad_one.astype(jnp.float32), value_one.astype(jnp.float32))
        row_delta = lax.optimization_barrier(jnp.sum(probabilities * grad_prob, axis=-1, keepdims=True))
        grad_scores = (probabilities * (grad_prob - row_delta)).astype(jnp.bfloat16).astype(jnp.float32)
        grad_query = jnp.einsum('rqk,kd->rqd', grad_scores, key_one.astype(jnp.float32)) * score_scale
        grad_key = jnp.einsum('rqk,rqd->kd', grad_scores, query_one.astype(jnp.float32)) * score_scale
        rounded = probabilities.astype(jnp.bfloat16).astype(jnp.float32)
        grad_value = jnp.einsum('rqk,rqd->kd', rounded, grad_one.astype(jnp.float32))
        return (grad_query, grad_key, grad_value)
    grad_query, grad_key, grad_value = lax.map(per_head, (query_heads, key_heads, value_heads, log_total, grad_heads))
    return (grad_query.transpose(2, 0, 1, 3).reshape(row_count, -1), grad_key.transpose(1, 0, 2).reshape(key_count, -1), grad_value.transpose(1, 0, 2).reshape(key_count, -1))

def norm_scale(stream):
    return lax.rsqrt(lax.optimization_barrier(jnp.mean(stream * stream, axis=-1, keepdims=True)) + EPS)

def norm_back(grad_normed, stream, scale_now, gain_now):
    weighted = grad_normed * gain_now.astype(jnp.float32)
    grad_gain = lax.optimization_barrier(jnp.sum(grad_normed * stream * scale_now, axis=0))
    grad_stream = scale_now * weighted - stream * scale_now ** 3 * lax.optimization_barrier(jnp.mean(weighted * stream, axis=-1, keepdims=True))
    return (grad_stream, grad_gain)

def forward(stream, params, position, allowed):
    query_weight, key_weight, value_weight, out_weight, gate_weight, up_weight, down_weight, gain_first, gain_second = params
    scale_first = norm_scale(stream)
    normed_first = (stream * scale_first * gain_first.astype(jnp.float32)).astype(jnp.bfloat16)
    query = rotate(product(normed_first, query_weight), position, 1.0).astype(jnp.bfloat16)
    key = rotate(product(normed_first, key_weight), position, 1.0).astype(jnp.bfloat16)
    value = product(normed_first, value_weight).astype(jnp.bfloat16)
    attended, log_total = attend(query, key, value, allowed)
    mid = stream + product(attended, out_weight)
    scale_second = norm_scale(mid)
    normed_second = (mid * scale_second * gain_second.astype(jnp.float32)).astype(jnp.bfloat16)
    gate = product(normed_second, gate_weight)
    up_part = product(normed_second, up_weight)
    hidden = (jax.nn.silu(gate) * up_part).astype(jnp.bfloat16)
    result = mid + product(hidden, down_weight)
    return (result, (stream, scale_first, normed_first, query, key, value, attended, log_total, mid, scale_second, normed_second, gate, up_part, hidden))

def backward(upstream, params, stored, position, allowed):
    query_weight, key_weight, value_weight, out_weight, gate_weight, up_weight, down_weight, gain_first, gain_second = params
    stream, scale_first, normed_first, query, key, value, attended, log_total, mid, scale_second, normed_second, gate, up_part, hidden = stored
    upstream_b = upstream.astype(jnp.bfloat16)
    grad_down = outer_sum(hidden, upstream_b)
    grad_hidden = transposed(upstream_b, down_weight)
    sigma = jax.nn.sigmoid(gate)
    grad_gate_in = (grad_hidden * up_part * sigma * (1.0 + gate * (1.0 - sigma))).astype(jnp.bfloat16)
    grad_up_in = (grad_hidden * gate * sigma).astype(jnp.bfloat16)
    grad_gate = outer_sum(normed_second, grad_gate_in)
    grad_up = outer_sum(normed_second, grad_up_in)
    grad_normed_second = transposed(grad_gate_in, gate_weight) + transposed(grad_up_in, up_weight)
    grad_mid_norm, grad_gain_second = norm_back(grad_normed_second, mid, scale_second, gain_second)
    grad_mid = upstream + grad_mid_norm
    grad_mid_b = grad_mid.astype(jnp.bfloat16)
    grad_out = outer_sum(attended, grad_mid_b)
    grad_attended = transposed(grad_mid_b, out_weight).astype(jnp.bfloat16)
    grad_query_raw, grad_key_raw, grad_value_raw = attend_back(query, key, value, allowed, log_total, grad_attended)
    grad_query_pre = rotate(grad_query_raw, position, -1.0).astype(jnp.bfloat16)
    grad_key_pre = rotate(grad_key_raw, position, -1.0).astype(jnp.bfloat16)
    grad_value_pre = grad_value_raw.astype(jnp.bfloat16)
    grad_query = outer_sum(normed_first, grad_query_pre)
    grad_key = outer_sum(normed_first, grad_key_pre)
    grad_value = outer_sum(normed_first, grad_value_pre)
    grad_normed_first = transposed(grad_query_pre, query_weight) + transposed(grad_key_pre, key_weight) + transposed(grad_value_pre, value_weight)
    grad_stream_norm, grad_gain_first = norm_back(grad_normed_first, stream, scale_first, gain_first)
    grad_stream = grad_mid + grad_stream_norm
    return (grad_stream, (grad_query, grad_key, grad_value, grad_out, grad_gate, grad_up, grad_down, grad_gain_first, grad_gain_second))

def reference(tokens, w_query, w_key, w_value, w_out, w_gate, w_up, w_down, gain_attn, gain_mlp, cotangent, piece_table, seq_lengths):
    all_weights = (w_query, w_key, w_value, w_out, w_gate, w_up, w_down, gain_attn, gain_mlp)

    def group_step(totals, inputs_now):
        token_rows, cotangent_rows, table_row, length_row = inputs_now
        logical, sequence, position = layout(table_row, length_row)
        allowed = (sequence[:, None] == sequence[None, :]) & (logical[None, :] <= logical[:, None])
        stream = token_rows.astype(jnp.float32)
        stored = []
        for layer_index in range(LAYERS):
            params = tuple((weight[layer_index] for weight in all_weights))
            stream, keep = forward(stream, params, position, allowed)
            stored.append(keep)
        upstream = cotangent_rows.astype(jnp.float32)
        gradients = [None] * LAYERS
        for layer_index in reversed(range(LAYERS)):
            params = tuple((weight[layer_index] for weight in all_weights))
            upstream, gradients[layer_index] = backward(upstream, params, stored[layer_index], position, allowed)
        stacked = tuple((jnp.stack([gradients[layer_index][member] for layer_index in range(LAYERS)]) for member in range(9)))
        totals = tuple((total + piece for total, piece in zip(totals, stacked)))
        return (totals, (stream.astype(jnp.bfloat16), upstream))
    initial = tuple((jnp.zeros(weight.shape, jnp.float32) for weight in all_weights))
    inputs = (tokens.reshape(N_FSDP, GROUP_TOK, D), cotangent.reshape(N_FSDP, GROUP_TOK, D), piece_table, seq_lengths)
    totals, (outputs, input_grads) = lax.scan(group_step, initial, inputs)
    return (outputs.reshape(TOKENS, D), input_grads.reshape(TOKENS, D), totals[0], totals[1], totals[2], totals[3], totals[4], totals[5], totals[6], totals[7], totals[8])
```

```python
import math

import jax
import jax.numpy as jnp
from jax import lax
from jax.sharding import PartitionSpec as P

H = 16
KV = 8
HD = 96
LAYERS = 2
PIECE = 128


EPS = 1e-05
THETA = 100000.0
NEG = -1e30


def layout(table_row, length_row):
    count = table_row.shape[0]
    slot_ids = jnp.arange(count, dtype=jnp.int32)
    owners = jnp.sum(
        jnp.where(table_row[:, None] == slot_ids[None, :], slot_ids[:, None], 0), axis=0
    )
    row_ids = jnp.arange(count * PIECE, dtype=jnp.int32)
    piece_of = row_ids // PIECE
    logical = (
        jnp.sum(jnp.where(piece_of[:, None] == slot_ids[None, :], owners[None, :], 0), axis=1)
        * PIECE
        + row_ids % PIECE
    )
    seq_ends = jnp.cumsum(length_row)
    passed = logical[:, None] >= seq_ends[None, :]
    sequence = jnp.sum(passed.astype(jnp.int32), axis=1)
    position = logical - jnp.sum(jnp.where(passed, length_row[None, :], 0), axis=1)
    return (logical, sequence, position)


def rotate(values, position, direction):
    row_count = values.shape[0]
    head_count = values.shape[1] // HD
    half_width = HD // 2
    frequency = jnp.exp(jnp.arange(half_width, dtype=jnp.float32) * (-2.0 * math.log(THETA) / HD))
    angles = position.astype(jnp.float32)[:, None] * frequency[None, :]
    cosine = jnp.cos(angles)[:, None, :]
    sine_part = direction * jnp.sin(angles)[:, None, :]
    shaped = values.reshape(row_count, head_count, HD)
    leading = shaped[..., :half_width]
    trailing = shaped[..., half_width:]
    return jnp.concatenate(
        [leading * cosine - trailing * sine_part, leading * sine_part + trailing * cosine], axis=-1
    ).reshape(row_count, head_count * HD)


def product(left, right):
    return jnp.dot(left, right, preferred_element_type=jnp.float32)


def outer_sum(left, right):
    return lax.dot_general(
        left, right, (((0,), (0,)), ((), ())), preferred_element_type=jnp.float32
    )


def transposed(left, right):
    return lax.dot_general(
        left, right, (((1,), (1,)), ((), ())), preferred_element_type=jnp.float32
    )


def split_heads(query, key, value):
    row_count = query.shape[0]
    key_count = key.shape[0]
    groups = key.shape[1] // HD
    shared = H // KV
    query_heads = query.reshape(row_count, groups, shared, HD).transpose(1, 2, 0, 3)
    key_heads = key.reshape(key_count, groups, HD).transpose(1, 0, 2)
    value_heads = value.reshape(key_count, groups, HD).transpose(1, 0, 2)
    return (query_heads, key_heads, value_heads)


def attend(query, key, value, allowed):
    row_count = query.shape[0]
    score_scale = 1.0 / math.sqrt(HD)
    query_heads, key_heads, value_heads = split_heads(query, key, value)

    def per_head(operands):
        query_one, key_one, value_one = operands
        scores = (
            jnp.einsum("rqd,kd->rqk", query_one, key_one, preferred_element_type=jnp.float32)
            * score_scale
        )
        scores = jnp.where(allowed[None], scores, NEG)
        row_max = jnp.max(scores, axis=-1, keepdims=True)
        log_total = row_max + jnp.log(jnp.sum(jnp.exp(scores - row_max), axis=-1, keepdims=True))
        probabilities = jnp.exp(scores - log_total).astype(jnp.bfloat16)
        result = jnp.einsum(
            "rqk,kd->rqd", probabilities, value_one, preferred_element_type=jnp.float32
        )
        return (result.astype(jnp.bfloat16), log_total[..., 0])

    attended, log_total = lax.map(per_head, (query_heads, key_heads, value_heads))
    return (attended.transpose(2, 0, 1, 3).reshape(row_count, -1), log_total)


def attend_back(query, key, value, allowed, log_total, grad_attended):
    row_count = query.shape[0]
    key_count = key.shape[0]
    score_scale = 1.0 / math.sqrt(HD)
    query_heads, key_heads, value_heads = split_heads(query, key, value)
    grad_heads = grad_attended.reshape(row_count, key.shape[1] // HD, H // KV, HD).transpose(
        1, 2, 0, 3
    )

    def per_head(operands):
        query_one, key_one, value_one, total_one, grad_one = operands
        scores = (
            jnp.einsum("rqd,kd->rqk", query_one, key_one, preferred_element_type=jnp.float32)
            * score_scale
        )
        scores = jnp.where(allowed[None], scores, NEG)
        probabilities = jnp.exp(scores - total_one[..., None])
        grad_prob = jnp.einsum(
            "rqd,kd->rqk", grad_one, value_one, preferred_element_type=jnp.float32
        )
        row_delta = jnp.sum(probabilities * grad_prob, axis=-1, keepdims=True)
        grad_scores = (probabilities * (grad_prob - row_delta)).astype(jnp.bfloat16)
        grad_query = (
            jnp.einsum("rqk,kd->rqd", grad_scores, key_one, preferred_element_type=jnp.float32)
            * score_scale
        )
        grad_key = (
            jnp.einsum("rqk,rqd->kd", grad_scores, query_one, preferred_element_type=jnp.float32)
            * score_scale
        )
        rounded = probabilities.astype(jnp.bfloat16)
        grad_value = jnp.einsum(
            "rqk,rqd->kd", rounded, grad_one, preferred_element_type=jnp.float32
        )
        return (grad_query, grad_key, grad_value)

    grad_query, grad_key, grad_value = lax.map(
        per_head, (query_heads, key_heads, value_heads, log_total, grad_heads)
    )
    return (
        grad_query.transpose(2, 0, 1, 3).reshape(row_count, -1),
        grad_key.transpose(1, 0, 2).reshape(key_count, -1),
        grad_value.transpose(1, 0, 2).reshape(key_count, -1),
    )


def norm_scale(stream):
    return lax.rsqrt(jnp.mean(stream * stream, axis=-1, keepdims=True) + EPS)


def norm_back(grad_normed, stream, scale_now, gain_now):
    weighted = grad_normed * gain_now.astype(jnp.float32)
    grad_gain = jnp.sum(grad_normed * stream * scale_now, axis=0)
    grad_stream = scale_now * weighted - stream * scale_now**3 * jnp.mean(
        weighted * stream, axis=-1, keepdims=True
    )
    return (grad_stream, grad_gain)


def fetch_layer(shards, layer_index):
    (
        query_weight,
        key_weight,
        value_weight,
        out_weight,
        gate_weight,
        up_weight,
        down_weight,
        gain_first,
        gain_second,
    ) = [item[layer_index] for item in shards]
    return (
        lax.all_gather(query_weight, "fsdp", axis=0, tiled=True),
        lax.all_gather(key_weight, "fsdp", axis=0, tiled=True),
        lax.all_gather(value_weight, "fsdp", axis=0, tiled=True),
        lax.all_gather(out_weight, "fsdp", axis=1, tiled=True),
        lax.all_gather(gate_weight, "fsdp", axis=0, tiled=True),
        lax.all_gather(up_weight, "fsdp", axis=0, tiled=True),
        lax.all_gather(down_weight, "fsdp", axis=1, tiled=True),
        lax.all_gather(gain_first, "fsdp", axis=0, tiled=True),
        lax.all_gather(gain_second, "fsdp", axis=0, tiled=True),
    )


def fetch_backward(shards, layer_index):
    (
        query_weight,
        key_weight,
        value_weight,
        out_weight,
        gate_weight,
        up_weight,
        down_weight,
        gain_first,
        gain_second,
    ) = [item[layer_index] for item in shards]
    return (
        lax.all_gather(query_weight, "fsdp", axis=0, tiled=True),
        lax.all_gather(key_weight, "fsdp", axis=0, tiled=True),
        lax.all_gather(value_weight, "fsdp", axis=0, tiled=True),
        lax.all_gather(out_weight, "fsdp", axis=1, tiled=True),
        lax.all_gather(gate_weight, "fsdp", axis=0, tiled=True),
        lax.all_gather(up_weight, "fsdp", axis=0, tiled=True),
        lax.all_gather(down_weight, "fsdp", axis=1, tiled=True),
        lax.all_gather(gain_first, "fsdp", axis=0, tiled=True),
        lax.all_gather(gain_second, "fsdp", axis=0, tiled=True),
    )


def forward(stream, params, position, allowed):
    (
        query_weight,
        key_weight,
        value_weight,
        out_weight,
        gate_weight,
        up_weight,
        down_weight,
        gain_first,
        gain_second,
    ) = params
    scale_first = norm_scale(stream)
    normed_first = (stream * scale_first * gain_first.astype(jnp.float32)).astype(jnp.bfloat16)
    query = rotate(product(normed_first, query_weight), position, 1.0).astype(jnp.bfloat16)
    key = rotate(product(normed_first, key_weight), position, 1.0).astype(jnp.bfloat16)
    value = product(normed_first, value_weight).astype(jnp.bfloat16)
    keys_all, values_all = (
        lax.all_gather(key, "ctx", axis=0, tiled=True),
        lax.all_gather(value, "ctx", axis=0, tiled=True),
    )
    attended, log_total = attend(query, keys_all, values_all, allowed)
    mid = stream + lax.psum(product(attended, out_weight), "tp")
    scale_second = norm_scale(mid)
    normed_second = (mid * scale_second * gain_second.astype(jnp.float32)).astype(jnp.bfloat16)
    gate = product(normed_second, gate_weight)
    up_part = product(normed_second, up_weight)
    hidden = (jax.nn.silu(gate) * up_part).astype(jnp.bfloat16)
    result = mid + lax.psum(product(hidden, down_weight), "tp")
    return (
        result,
        (
            stream,
            scale_first,
            normed_first,
            query,
            keys_all,
            values_all,
            attended,
            log_total,
            mid,
            scale_second,
            normed_second,
            gate,
            up_part,
            hidden,
        ),
    )


def backward(upstream, params, stored, position, allowed):
    (
        query_weight,
        key_weight,
        value_weight,
        out_weight,
        gate_weight,
        up_weight,
        down_weight,
        gain_first,
        gain_second,
    ) = params
    (
        stream,
        scale_first,
        normed_first,
        query,
        keys_all,
        values_all,
        attended,
        log_total,
        mid,
        scale_second,
        normed_second,
        gate,
        up_part,
        hidden,
    ) = stored
    upstream_b = upstream.astype(jnp.bfloat16)
    grad_down = outer_sum(hidden, upstream_b)
    grad_hidden = transposed(upstream_b, down_weight)
    sigma = jax.nn.sigmoid(gate)
    grad_gate_in = (grad_hidden * up_part * sigma * (1.0 + gate * (1.0 - sigma))).astype(
        jnp.bfloat16
    )
    grad_up_in = (grad_hidden * gate * sigma).astype(jnp.bfloat16)
    grad_gate = outer_sum(normed_second, grad_gate_in)
    grad_up = outer_sum(normed_second, grad_up_in)
    grad_normed_second = lax.psum(
        (transposed(grad_gate_in, gate_weight) + transposed(grad_up_in, up_weight)).astype(
            jnp.bfloat16
        ),
        "tp",
    ).astype(jnp.float32)
    grad_mid_norm, grad_gain_second = norm_back(grad_normed_second, mid, scale_second, gain_second)
    grad_mid = upstream + grad_mid_norm
    grad_mid_b = grad_mid.astype(jnp.bfloat16)
    grad_out = outer_sum(attended, grad_mid_b)
    grad_attended = transposed(grad_mid_b, out_weight).astype(jnp.bfloat16)
    grad_query_raw, grad_key_all, grad_value_all = attend_back(
        query, keys_all, values_all, allowed, log_total, grad_attended
    )
    grad_key_raw, grad_value_raw = (
        lax.psum_scatter(
            grad_key_all.astype(jnp.bfloat16), "ctx", scatter_dimension=0, tiled=True
        ).astype(jnp.float32),
        lax.psum_scatter(
            grad_value_all.astype(jnp.bfloat16), "ctx", scatter_dimension=0, tiled=True
        ).astype(jnp.float32),
    )
    grad_query_pre = rotate(grad_query_raw, position, -1.0).astype(jnp.bfloat16)
    grad_key_pre = rotate(grad_key_raw, position, -1.0).astype(jnp.bfloat16)
    grad_value_pre = grad_value_raw.astype(jnp.bfloat16)
    grad_query = outer_sum(normed_first, grad_query_pre)
    grad_key = outer_sum(normed_first, grad_key_pre)
    grad_value = outer_sum(normed_first, grad_value_pre)
    grad_normed_first = lax.psum(
        (
            transposed(grad_query_pre, query_weight)
            + transposed(grad_key_pre, key_weight)
            + transposed(grad_value_pre, value_weight)
        ).astype(jnp.bfloat16),
        "tp",
    ).astype(jnp.float32)
    grad_stream_norm, grad_gain_first = norm_back(
        grad_normed_first, stream, scale_first, gain_first
    )
    grad_stream = grad_mid + grad_stream_norm
    return (
        grad_stream,
        (
            grad_query,
            grad_key,
            grad_value,
            grad_out,
            grad_gate,
            grad_up,
            grad_down,
            grad_gain_first,
            grad_gain_second,
        ),
    )


def reduce_gradients(gradients):
    (
        grad_query,
        grad_key,
        grad_value,
        grad_out,
        grad_gate,
        grad_up,
        grad_down,
        grad_gain_first,
        grad_gain_second,
    ) = gradients
    shares = (
        lax.psum_scatter(
            grad_query.astype(jnp.bfloat16), "fsdp", scatter_dimension=0, tiled=True
        ).astype(jnp.float32),
        lax.psum_scatter(
            grad_key.astype(jnp.bfloat16), "fsdp", scatter_dimension=0, tiled=True
        ).astype(jnp.float32),
        lax.psum_scatter(
            grad_value.astype(jnp.bfloat16), "fsdp", scatter_dimension=0, tiled=True
        ).astype(jnp.float32),
        lax.psum_scatter(
            grad_out.astype(jnp.bfloat16), "fsdp", scatter_dimension=1, tiled=True
        ).astype(jnp.float32),
        lax.psum_scatter(
            grad_gate.astype(jnp.bfloat16), "fsdp", scatter_dimension=0, tiled=True
        ).astype(jnp.float32),
        lax.psum_scatter(
            grad_up.astype(jnp.bfloat16), "fsdp", scatter_dimension=0, tiled=True
        ).astype(jnp.float32),
        lax.psum_scatter(
            grad_down.astype(jnp.bfloat16), "fsdp", scatter_dimension=1, tiled=True
        ).astype(jnp.float32),
        lax.psum_scatter(
            grad_gain_first.astype(jnp.bfloat16), "fsdp", scatter_dimension=0, tiled=True
        ).astype(jnp.float32),
        lax.psum_scatter(
            grad_gain_second.astype(jnp.bfloat16), "fsdp", scatter_dimension=0, tiled=True
        ).astype(jnp.float32),
    )
    return (
        lax.psum(shares[0].astype(jnp.bfloat16), "ctx").astype(jnp.float32),
        lax.psum(shares[1].astype(jnp.bfloat16), "ctx").astype(jnp.float32),
        lax.psum(shares[2].astype(jnp.bfloat16), "ctx").astype(jnp.float32),
        lax.psum(shares[3].astype(jnp.bfloat16), "ctx").astype(jnp.float32),
        lax.psum(shares[4].astype(jnp.bfloat16), "ctx").astype(jnp.float32),
        lax.psum(shares[5].astype(jnp.bfloat16), "ctx").astype(jnp.float32),
        lax.psum(shares[6].astype(jnp.bfloat16), "ctx").astype(jnp.float32),
        lax.psum(shares[7].astype(jnp.bfloat16), "ctx").astype(jnp.float32),
        lax.psum(shares[8].astype(jnp.bfloat16), "ctx").astype(jnp.float32),
    )


def per_device(
    tokens,
    w_query,
    w_key,
    w_value,
    w_out,
    w_gate,
    w_up,
    w_down,
    gain_attn,
    gain_mlp,
    cotangent,
    piece_table,
    seq_lengths,
):
    group_index = lax.axis_index("fsdp")
    piece_index = lax.axis_index("ctx")
    table_row = lax.dynamic_index_in_dim(piece_table, group_index, 0, keepdims=False)
    length_row = lax.dynamic_index_in_dim(seq_lengths, group_index, 0, keepdims=False)
    logical, sequence, position = layout(table_row, length_row)
    local_count = tokens.shape[0]
    first_row = piece_index * local_count
    own_logical = lax.dynamic_slice_in_dim(logical, first_row, local_count)
    own_sequence = lax.dynamic_slice_in_dim(sequence, first_row, local_count)
    own_position = lax.dynamic_slice_in_dim(position, first_row, local_count)
    allowed = (own_sequence[:, None] == sequence[None, :]) & (
        logical[None, :] <= own_logical[:, None]
    )
    shards = (w_query, w_key, w_value, w_out, w_gate, w_up, w_down, gain_attn, gain_mlp)
    stream = tokens.astype(jnp.float32)
    stored = []
    for layer_index in range(LAYERS):
        params = fetch_layer(shards, layer_index)
        stream, keep = forward(stream, params, own_position, allowed)
        stored.append(keep)
    upstream = cotangent.astype(jnp.float32)
    reduced = [None] * LAYERS
    for layer_index in reversed(range(LAYERS)):
        params = fetch_backward(shards, layer_index)
        upstream, gradients = backward(upstream, params, stored[layer_index], own_position, allowed)
        reduced[layer_index] = reduce_gradients(gradients)
    stacked = [
        jnp.stack([reduced[layer_index][member] for layer_index in range(LAYERS)])
        for member in range(9)
    ]
    return (
        stream.astype(jnp.bfloat16),
        upstream,
        stacked[0],
        stacked[1],
        stacked[2],
        stacked[3],
        stacked[4],
        stacked[5],
        stacked[6],
        stacked[7],
        stacked[8],
    )


CORE_SWAP = ((0, 1), (1, 0), (2, 3), (3, 2))
CHIP_SWAP = ((0, 2), (2, 0), (1, 3), (3, 1))
PAIR_SWAP = ((0, 1), (1, 0))


def fast_fits(shape):
    return shape["ctx"] == 2 and shape["tp"] == 4 and KV % (2 * shape["tp"]) == 0


def core_swap(values):
    return lax.ppermute(values, "tp", CORE_SWAP)


def chip_swap(values):
    return lax.ppermute(values, "tp", CHIP_SWAP)


def pair_swap(values):
    return lax.ppermute(values, "ctx", PAIR_SWAP)


def ring_shift(values):
    count = lax.axis_size("fsdp")
    return lax.ppermute(values, "fsdp", [(i, (i + 1) % count) for i in range(count)])


def rounded(values):
    return lax.reduce_precision(values, 8, 7).astype(jnp.bfloat16)


def ordered(flag, own, other, axis):
    return jnp.where(
        flag,
        jnp.concatenate([own, other], axis=axis),
        jnp.concatenate([other, own], axis=axis),
    )


def relative_columns(values, group_index):
    count = lax.axis_size("fsdp")
    width = values.shape[1] // count
    return jnp.concatenate(
        [
            lax.dynamic_slice_in_dim(values, (group_index - step) % count * width, width, 1)
            for step in range(count)
        ],
        axis=1,
    )


absolute_columns = relative_columns


def relative_rows(values, core):
    half = values.shape[0] // 2
    return jnp.concatenate(
        [
            lax.dynamic_slice_in_dim(values, core * half, half, 0),
            lax.dynamic_slice_in_dim(values, (1 - core) * half, half, 0),
        ],
        axis=0,
    )


def pack_layer(shards, layer_index, first):
    query, key, value, out, gate, up, down = [item[layer_index] for item in shards]

    def half(values, side):
        width = values.shape[1] // 2
        return values[:, side * width : (side + 1) * width]

    packs = []
    for members in ((query, key, value, out.T), (gate, up, down.T)):
        low = jnp.concatenate([half(member, 0) for member in members], axis=1)
        high = jnp.concatenate([half(member, 1) for member in members], axis=1)
        packs.append((jnp.where(first, low, high), jnp.where(first, high, low)))
    return packs


def gather_pack(pack):
    own, other = pack
    own_parts = [own]
    for _ in range(lax.axis_size("fsdp") - 1):
        own_parts.append(ring_shift(own_parts[-1]))
    other_parts = [other] + [pair_swap(part) for part in own_parts[1:]]
    return (jnp.concatenate(own_parts, axis=0), jnp.concatenate(other_parts, axis=0))


def tp_sum(make, half, narrow):
    away = make(slice(half, None))
    away = core_swap(rounded(away) if narrow else away)
    total = rounded(make(slice(0, half)) + away.astype(jnp.float32))
    return total.astype(jnp.float32) + chip_swap(total).astype(jnp.float32)


def both_rows(values):
    return jnp.concatenate([values, core_swap(values)], axis=0)


def turn(values, cosine, sine):
    half = HD // 2
    parts = []
    for start in range(0, values.shape[1], HD):
        leading = values[:, start : start + half]
        trailing = values[:, start + half : start + HD]
        parts.append(leading * cosine - trailing * sine)
        parts.append(leading * sine + trailing * cosine)
    return jnp.concatenate(parts, axis=1)


def fast_attend(query, key, value, allowed):
    rows = query.shape[0]
    heads = query.reshape(rows, -1, HD).transpose(1, 0, 2)
    scores = jnp.einsum("rqd,kd->rqk", heads, key, preferred_element_type=jnp.float32)
    scores = jnp.where(allowed[None], scores * (1.0 / math.sqrt(HD)), NEG)
    row_max = jnp.max(scores, axis=-1, keepdims=True)
    log_total = row_max + jnp.log(jnp.sum(jnp.exp(scores - row_max), axis=-1, keepdims=True))
    probabilities = jnp.exp(scores - log_total).astype(jnp.bfloat16)
    result = jnp.einsum("rqk,kd->rqd", probabilities, value, preferred_element_type=jnp.float32)
    return (result.astype(jnp.bfloat16).transpose(1, 0, 2).reshape(rows, -1), log_total)


def fast_attend_back(query, key, value, allowed, log_total, grad_attended):
    rows = query.shape[0]
    scale = 1.0 / math.sqrt(HD)
    heads = query.reshape(rows, -1, HD).transpose(1, 0, 2)
    grads = grad_attended.reshape(rows, -1, HD).transpose(1, 0, 2)
    scores = jnp.einsum("rqd,kd->rqk", heads, key, preferred_element_type=jnp.float32) * scale
    scores = jnp.where(allowed[None], scores, NEG)
    probabilities = jnp.exp(scores - log_total)
    grad_prob = jnp.einsum("rqd,kd->rqk", grads, value, preferred_element_type=jnp.float32)
    row_delta = jnp.sum(probabilities * grad_prob, axis=-1, keepdims=True)
    grad_scores = (probabilities * (grad_prob - row_delta)).astype(jnp.bfloat16)
    grad_query = (
        jnp.einsum("rqk,kd->rqd", grad_scores, key, preferred_element_type=jnp.float32) * scale
    )
    grad_key = (
        jnp.einsum("rqk,rqd->kd", grad_scores, heads, preferred_element_type=jnp.float32) * scale
    )
    grad_value = jnp.einsum(
        "rqk,rqd->kd", probabilities.astype(jnp.bfloat16), grads, preferred_element_type=jnp.float32
    )
    return (grad_query.transpose(1, 0, 2).reshape(rows, -1), grad_key, grad_value)


def normed(stream, scale, gain):
    return (stream * scale * gain.astype(jnp.float32)).astype(jnp.bfloat16)


def ring_reduce(parts):
    moving = rounded(parts[1])
    for part in parts[2:] + parts[:1]:
        moving = rounded(ring_shift(moving).astype(jnp.float32) + part.astype(jnp.float32))
    return moving


def fast_device(
    tokens,
    w_query,
    w_key,
    w_value,
    w_out,
    w_gate,
    w_up,
    w_down,
    gain_attn,
    gain_mlp,
    cotangent,
    piece_table,
    seq_lengths,
):
    group_index = lax.axis_index("fsdp")
    piece_index = lax.axis_index("ctx")
    core = lax.axis_index("tp") % 2
    first = piece_index == 0
    front = core == 0
    blocks = lax.axis_size("fsdp")
    shards = (w_query, w_key, w_value, w_out, w_gate, w_up, w_down)
    packs = [pack_layer(shards, layer_index, first) for layer_index in range(LAYERS)]
    gain_parts = [jnp.concatenate([gain_attn, gain_mlp], axis=0)]
    for _ in range(blocks - 1):
        gain_parts.append(ring_shift(gain_parts[-1]))
    gains = jnp.concatenate(gain_parts, axis=1)

    table_row = lax.dynamic_index_in_dim(piece_table, group_index, 0, keepdims=False)
    length_row = lax.dynamic_index_in_dim(seq_lengths, group_index, 0, keepdims=False)
    logical, sequence, position = layout(table_row, length_row)
    rows = tokens.shape[0]
    half = rows // 2

    def rows_of(values, owner):
        return relative_rows(lax.dynamic_slice_in_dim(values, owner * rows, rows), core)

    def key_rows(values):
        return jnp.concatenate([rows_of(values, piece_index), rows_of(values, 1 - piece_index)])

    own_logical = rows_of(logical, piece_index)
    own_sequence = rows_of(sequence, piece_index)
    own_position = rows_of(position, piece_index)
    allowed = (own_sequence[:, None] == key_rows(sequence)[None, :]) & (
        key_rows(logical)[None, :] <= own_logical[:, None]
    )
    frequency = jnp.exp(jnp.arange(HD // 2, dtype=jnp.float32) * (-2.0 * math.log(THETA) / HD))
    angles = own_position.astype(jnp.float32)[:, None] * frequency[None, :]
    cosine = jnp.cos(angles)
    sine = jnp.sin(angles)

    attn_width = w_query.shape[2] // 2
    kv_width = w_key.shape[2] // 2
    qk_width = attn_width + kv_width
    qkv_width = qk_width + kv_width
    hidden_width = w_gate.shape[2] // 2

    tokens_full = relative_rows(relative_columns(tokens, group_index), core).astype(jnp.float32)
    stream = tokens_full[:half]
    stored = []
    for layer_index in range(LAYERS):
        attn = gather_pack(packs[layer_index][0])
        mlp = gather_pack(packs[layer_index][1])
        gain_first = gains[layer_index]
        gain_second = gains[LAYERS + layer_index]
        scale_first = norm_scale(stream)
        if layer_index == 0:
            normed_first = normed(tokens_full, norm_scale(tokens_full), gain_first)
            normed_first_half = normed_first[:half]
        else:
            normed_first_half = normed(stream, scale_first, gain_first)
            normed_first = both_rows(normed_first_half)
        queries, keys, values = [], [], []
        for side in range(2):
            mixed = product(normed_first, attn[side][:, :qkv_width])
            turned = turn(mixed[:, :qk_width], cosine, sine).astype(jnp.bfloat16)
            queries.append(turned[:, :attn_width])
            keys.append(turned[:, attn_width:])
            values.append(mixed[:, qk_width:].astype(jnp.bfloat16))
        peer = pair_swap(jnp.concatenate([keys[1], keys[0], values[1], values[0]], axis=1))
        peers = [peer[:, i * kv_width : (i + 1) * kv_width] for i in range(4)]
        keys = [jnp.concatenate([keys[side], peers[side]], axis=0) for side in range(2)]
        values = [jnp.concatenate([values[side], peers[2 + side]], axis=0) for side in range(2)]
        attended, log_total = [], []
        for side in range(2):
            result, total = fast_attend(queries[side], keys[side], values[side], allowed)
            attended.append(result)
            log_total.append(total)

        def out_rows(chosen):
            return transposed(attended[0][chosen], attn[0][:, qkv_width:]) + transposed(
                attended[1][chosen], attn[1][:, qkv_width:]
            )

        mid = stream + tp_sum(out_rows, half, False)
        scale_second = norm_scale(mid)
        normed_second_half = normed(mid, scale_second, gain_second)
        normed_second = both_rows(normed_second_half)
        gate, up_part, hidden = [], [], []
        for side in range(2):
            mixed = product(normed_second, mlp[side][:, : 2 * hidden_width])
            gate.append(mixed[:, :hidden_width])
            up_part.append(mixed[:, hidden_width:])
            hidden.append((jax.nn.silu(gate[side]) * up_part[side]).astype(jnp.bfloat16))

        def down_rows(chosen):
            return transposed(hidden[0][chosen], mlp[0][:, 2 * hidden_width :]) + transposed(
                hidden[1][chosen], mlp[1][:, 2 * hidden_width :]
            )

        result = mid + tp_sum(down_rows, half, False)
        stored.append(
            (
                attn,
                mlp,
                stream,
                scale_first,
                normed_first,
                normed_first_half,
                queries,
                keys,
                values,
                attended,
                log_total,
                mid,
                scale_second,
                normed_second,
                normed_second_half,
                gate,
                up_part,
                hidden,
            )
        )
        stream = result
    output = stream.astype(jnp.bfloat16)

    cotangent_full = relative_rows(relative_columns(cotangent, group_index), core)
    upstream = cotangent_full[:half].astype(jnp.float32)
    attn_shares = [None] * LAYERS
    mlp_shares = [None] * LAYERS
    gain_grads = [None] * (2 * LAYERS)
    for layer_index in reversed(range(LAYERS)):
        (
            attn,
            mlp,
            stream,
            scale_first,
            normed_first,
            normed_first_half,
            queries,
            keys,
            values,
            attended,
            log_total,
            mid,
            scale_second,
            normed_second,
            normed_second_half,
            gate,
            up_part,
            hidden,
        ) = stored[layer_index]
        upstream_half = upstream.astype(jnp.bfloat16)
        if layer_index == LAYERS - 1:
            upstream_b = cotangent_full
        else:
            upstream_b = both_rows(upstream_half)
        grad_in = []
        for side in range(2):
            grad_hidden = product(upstream_b, mlp[side][:, 2 * hidden_width :])
            sigma = jax.nn.sigmoid(gate[side])
            grad_gate_in = grad_hidden * up_part[side] * sigma * (1.0 + gate[side] * (1.0 - sigma))
            grad_up_in = grad_hidden * gate[side] * sigma
            grad_in.append(
                jnp.concatenate([grad_gate_in, grad_up_in], axis=1).astype(jnp.bfloat16)
            )

        def second_rows(chosen):
            return transposed(grad_in[0][chosen], mlp[0][:, : 2 * hidden_width]) + transposed(
                grad_in[1][chosen], mlp[1][:, : 2 * hidden_width]
            )

        grad_normed_second = tp_sum(second_rows, half, True)
        grad_mid_norm, gain_grads[LAYERS + layer_index] = norm_back(
            grad_normed_second, mid, scale_second, gains[LAYERS + layer_index]
        )
        grad_mid = upstream + grad_mid_norm
        grad_mid_half = grad_mid.astype(jnp.bfloat16)
        grad_mid_b = both_rows(grad_mid_half)

        normed_pair = jnp.concatenate(
            [normed_second, both_rows(pair_swap(normed_second_half))], axis=0
        )
        upstream_pair = jnp.concatenate([upstream_b, both_rows(pair_swap(upstream_half))], axis=0)
        grad_in_pair = jnp.concatenate([grad_in[0], pair_swap(grad_in[1])], axis=0)
        hidden_pair = jnp.concatenate([hidden[0], pair_swap(hidden[1])], axis=0)
        width = normed_second.shape[1] // blocks
        mlp_parts = []
        for block in range(blocks):
            columns = slice(block * width, (block + 1) * width)
            mlp_parts.append(
                jnp.concatenate(
                    [
                        outer_sum(normed_pair[:, columns], grad_in_pair),
                        outer_sum(upstream_pair[:, columns], hidden_pair),
                    ],
                    axis=1,
                )
            )
        mlp_shares[layer_index] = ring_reduce(mlp_parts)

        grad_query, grad_key, grad_value = [], [], []
        for side in range(2):
            grad_attended = product(grad_mid_b, attn[side][:, qkv_width:]).astype(jnp.bfloat16)
            back = fast_attend_back(
                queries[side], keys[side], values[side], allowed, log_total[side], grad_attended
            )
            grad_query.append(back[0])
            grad_key.append(back[1])
            grad_value.append(back[2])
        returned = pair_swap(
            jnp.concatenate(
                [grad_key[1][rows:], grad_key[0][rows:], grad_value[1][rows:], grad_value[0][rows:]],
                axis=1,
            ).astype(jnp.bfloat16)
        ).astype(jnp.float32)
        grad_mixed = []
        for side in range(2):
            key_sum = (
                grad_key[side][:rows].astype(jnp.bfloat16).astype(jnp.float32)
                + returned[:, side * kv_width : (side + 1) * kv_width]
            )
            value_sum = (
                grad_value[side][:rows].astype(jnp.bfloat16).astype(jnp.float32)
                + returned[:, (2 + side) * kv_width : (3 + side) * kv_width]
            )
            turned = turn(jnp.concatenate([grad_query[side], key_sum], axis=1), cosine, -sine)
            grad_mixed.append(
                jnp.concatenate([turned, value_sum], axis=1).astype(jnp.bfloat16)
            )

        def first_rows(chosen):
            return transposed(grad_mixed[0][chosen], attn[0][:, :qkv_width]) + transposed(
                grad_mixed[1][chosen], attn[1][:, :qkv_width]
            )

        grad_normed_first = tp_sum(first_rows, half, True)
        grad_stream_norm, gain_grads[layer_index] = norm_back(
            grad_normed_first, stream, scale_first, gains[layer_index]
        )
        upstream = grad_mid + grad_stream_norm

        first_pair = jnp.concatenate(
            [normed_first, both_rows(pair_swap(normed_first_half))], axis=0
        )
        mixed_pair = jnp.concatenate([grad_mixed[0], pair_swap(grad_mixed[1])], axis=0)
        out_other = pair_swap(rounded(outer_sum(grad_mid_b, attended[1]))).astype(jnp.float32)
        out_own = outer_sum(grad_mid_b, attended[0]) + out_other
        attn_parts = []
        for block in range(blocks):
            columns = slice(block * width, (block + 1) * width)
            attn_parts.append(
                jnp.concatenate(
                    [outer_sum(first_pair[:, columns], mixed_pair), out_own[columns]], axis=1
                )
            )
        attn_shares[layer_index] = ring_reduce(attn_parts)

    gain_sum = jnp.stack(gain_grads)
    gain_sum = gain_sum + core_swap(gain_sum)
    gain_sum = gain_sum + pair_swap(gain_sum)
    gain_share = ring_reduce(
        [gain_sum[:, block * width : (block + 1) * width] for block in range(blocks)]
    ).astype(jnp.float32)

    bounds_attn = (0, attn_width, qk_width, qkv_width, qkv_width + attn_width)
    bounds_mlp = (0, hidden_width, 2 * hidden_width, 3 * hidden_width)
    grads = []
    for shares, bounds in ((attn_shares, bounds_attn), (mlp_shares, bounds_mlp)):
        others = [pair_swap(share) for share in shares]
        for low, high in zip(bounds[:-1], bounds[1:]):
            grads.append(
                [
                    ordered(first, share[:, low:high], other[:, low:high], 1).astype(jnp.float32)
                    for share, other in zip(shares, others)
                ]
            )
    grad_q, grad_k, grad_v, grad_o, grad_g, grad_u, grad_d = grads
    grad_o = [member.T for member in grad_o]
    grad_d = [member.T for member in grad_d]
    output = absolute_columns(ordered(front, output, core_swap(output), 0), group_index)
    input_grad = absolute_columns(ordered(front, upstream, core_swap(upstream), 0), group_index)
    return (
        output,
        input_grad,
        jnp.stack(grad_q),
        jnp.stack(grad_k),
        jnp.stack(grad_v),
        jnp.stack(grad_o),
        jnp.stack(grad_g),
        jnp.stack(grad_u),
        jnp.stack(grad_d),
        gain_share[:LAYERS],
        gain_share[LAYERS:],
    )


def solution(mesh):
    body = fast_device if fast_fits(mesh.shape) else per_device
    placed = (
        P(("fsdp", "ctx"), None),
        P(None, "fsdp", "tp"),
        P(None, "fsdp", "tp"),
        P(None, "fsdp", "tp"),
        P(None, "tp", "fsdp"),
        P(None, "fsdp", "tp"),
        P(None, "fsdp", "tp"),
        P(None, "tp", "fsdp"),
        P(None, "fsdp"),
        P(None, "fsdp"),
        P(("fsdp", "ctx"), None),
        P(),
        P(),
    )
    return jax.shard_map(
        body,
        mesh=mesh,
        in_specs=placed,
        out_specs=(
            P(("fsdp", "ctx"), None),
            P(("fsdp", "ctx"), None),
            P(None, "fsdp", "tp"),
            P(None, "fsdp", "tp"),
            P(None, "fsdp", "tp"),
            P(None, "tp", "fsdp"),
            P(None, "fsdp", "tp"),
            P(None, "fsdp", "tp"),
            P(None, "tp", "fsdp"),
            P(None, "fsdp"),
            P(None, "fsdp"),
        ),
        check_vma=False,
    )
```
